32 devices in a mesh: section: 2 (over core), shard: 2 (over x), ctx: 4 (over z), tp: 2 (over y).
Axes of the slice: x: 2, y: 2, z: 4, core: 2. Of those that a mesh axis runs over, the one named last changes fastest.
Arguments:
- boundary: float32 [2, 2, 1024, 1024], P('section', 'shard', 'ctx'), may hold values from -6 to 6
- segments: int32 [2, 1024], P('shard'), may hold values from 0 to 3, never falling along the last dimension, each value on 1 to 512 neighbouring positions
- norm_gain: float32 [2, 1024], P('section'), may hold values from 0.5 to 1.5
- inner_proj: bfloat16 [2, 1024, 2, 2048], P('section', 'shard', None, 'tp'), may hold values from -0.1875 to 0.1875
- state_proj: bfloat16 [2, 1024, 288], P('section', 'shard'), may hold values from -0.1875 to 0.1875
- conv_inner: float32 [2, 4, 2048], P('section', None, 'tp'), may hold values from -3 to 3
- conv_inner_bias: float32 [2, 2048], P('section', 'tp'), may hold values from -0.5 to 0.5
- conv_state: float32 [2, 4, 256], P('section'), may hold values from -3 to 3
- conv_state_bias: float32 [2, 256], P('section'), may hold values from -0.5 to 0.5
- step_bias: float32 [2, 32], P('section', 'tp'), may hold values from -7 to -5
- decay_log: float32 [2, 32], P('section', 'tp'), may hold values from -2 to 3
- skip_gain: float32 [2, 32], P('section', 'tp'), may hold values from 0.5 to 1.5
- gate_gain: float32 [2, 2048], P('section', 'tp'), may hold values from 0.5 to 1.5
- output_proj: bfloat16 [2, 1024, 2048], P('section', 'shard', 'tp'), may hold values from -0.125 to 0.125
Outputs:
- boundary_out: float32 [2, 2, 1024, 1024], P('section', 'shard', 'ctx')
- grad_norm_gain: float32 [2, 1024], P('section')
- grad_inner_proj: float32 [2, 1024, 2, 2048], P('section', ('shard', 'ctx'), None, 'tp')
- grad_state_proj: float32 [2, 1024, 288], P('section', ('shard', 'ctx'))
- grad_conv_inner: float32 [2, 4, 2048], P('section')
- grad_conv_inner_bias: float32 [2, 2048], P('section')
- grad_conv_state: float32 [2, 4, 256], P('section')
- grad_conv_state_bias: float32 [2, 256], P('section')
- grad_step_bias: float32 [2, 32], P('section')
- grad_decay_log: float32 [2, 32], P('section')
- grad_skip_gain: float32 [2, 32], P('section')
- grad_gate_gain: float32 [2, 2048], P('section')
- grad_output_proj: float32 [2, 1024, 2048], P('section', ('shard', 'ctx'), 'tp')
The draws below stay inside these ranges and needn't reach their ends.
Inputs may be any that keep to these rules, and one draw needn't show every extreme that they name: `segments`: in each sequence the numbers start at 0 and never fall; each document has 1 to 512 tokens, and one of them exactly 512.
All inputs are finite; a program needn't handle non-finite values.
Results may differ from the reference program's by a relative error of at most 0.02.
Values may be sent and summed in bfloat16 or wider, within the bound.
A program may use at most 128 MiB of HBM per device.

```python
import math
import jax
import jax.numpy as jnp
import numpy as np
from jax import lax

D = 1024
E = 2048
HEADS = 32
HEAD_DIM = 64
STATE = 128
CONV = 4
SPAN = 256
CPD = 1
LEN = 1024
SEQS = 2


def block_levels(stream_key, dims, split, least, top_value):
    def one(position, blocks):
        draws = jax.random.uniform(jax.random.fold_in(jax.random.fold_in(stream_key, 6), position), (blocks,), jnp.float32, least / len(split), top_value / len(split))
        return jnp.repeat(jnp.exp(draws), dims[position] // blocks).reshape((-1,) + (1,) * (len(dims) - position - 1))

    factor_of = one(*split[0])
    for cut in split[1:]:
        factor_of = factor_of * one(*cut)
    return factor_of


def profile(count, total, limit, slope):
    portions = [(1 << 20) // math.isqrt(standing ** slope) + 1 for standing in range(2, count + 1)]
    surplus, counts = total - limit - (count - 1), [1] * (count - 1)
    while surplus > 0:
        free = [i for i in range(count - 1) if counts[i] < limit]
        pool, remaining = sum([portions[i] for i in free]), surplus
        for i in free:
            extra = min(limit - counts[i], max(1, remaining * portions[i] // pool), surplus)
            counts[i] = counts[i] + extra
            surplus = surplus - extra
    return np.array([limit] + counts)


def uneven_parts(own_key, number_of, total, most, lean):
    if number_of == 2:
        one = jax.random.randint(own_key, (), max(1, total - most), min(most, total - 1) + 1)
        return jnp.stack([one, total - one])
    sizes = jnp.asarray(profile(number_of, total, most, lean), jnp.int32)
    pairs = (number_of - 1) // 2
    source_of, sink = sizes[1:1 + 2 * pairs:2], sizes[2:2 + 2 * pairs:2]
    margin = jnp.minimum(source_of - 1, most - sink)
    passed = jax.random.randint(jax.random.fold_in(own_key, 1), (pairs,), 0, 1 << 20) % (margin + 1)
    sizes = sizes.at[1:1 + 2 * pairs:2].set(source_of - passed).at[2:2 + 2 * pairs:2].set(sink + passed)
    return sizes[jax.random.permutation(jax.random.fold_in(own_key, 2), number_of)]


def bell_draw(own_key, dims, scale, bound, cuts=(), dtype=jnp.bfloat16):
    gain = block_levels(own_key, dims, cuts, -0.22, 0.18) if cuts else 1.0
    values = jax.random.normal(own_key, dims, jnp.float32) * scale * gain
    return jnp.minimum(jnp.maximum(values, -bound), bound).astype(dtype)


def setup_inputs(seed: int = 0) -> dict:
    splits = jax.random.split(jax.random.key(seed), 15)
    return {
        "boundary": bell_draw(splits[0], (2, SEQS, LEN, D), 1.0, 6.0, ((0, 2), (1, 2), (2, 4)), jnp.float32),
        "segments": jax.vmap(lambda own: jnp.searchsorted(jnp.cumsum(uneven_parts(own, 4 * CPD, LEN, LEN // 2, 1)), jnp.arange(LEN), side="right"))(jax.random.split(splits[1], SEQS)).reshape((SEQS, LEN)).astype(jnp.int32),
        "norm_gain": jnp.clip(1.0 + 0.1 * jax.random.normal(splits[2], (2, D), jnp.float32), 0.5, 1.5),
        "inner_proj": bell_draw(splits[3], (2, D, 2, E), D ** -0.5, 0.1875, ((0, 2), (1, 2), (3, 2))),
        "state_proj": bell_draw(splits[4], (2, D, 2 * STATE + HEADS), D ** -0.5, 0.1875, ((0, 2), (1, 2))),
        "conv_inner": bell_draw(splits[5], (2, CONV, E), CONV ** -0.5, 3.0, ((0, 2), (2, 2)), jnp.float32),
        "conv_inner_bias": jnp.clip(jax.random.uniform(splits[6], (2, E), jnp.float32, -0.5, 0.5) * block_levels(splits[6], (2, E), ((0, 2), (1, 2)), -0.4, 0.0), -0.5, 0.5),
        "conv_state": bell_draw(splits[7], (2, CONV, 2 * STATE), CONV ** -0.5, 3.0, ((0, 2),), jnp.float32),
        "conv_state_bias": jnp.clip(jax.random.uniform(splits[8], (2, 2 * STATE), jnp.float32, -0.5, 0.5) * block_levels(splits[8], (2, 2 * STATE), ((0, 2),), -0.4, 0.0), -0.5, 0.5),
        "step_bias": jnp.clip(-7.0 + 2.0 * jax.random.uniform(splits[9], (2, HEADS), jnp.float32) ** block_levels(splits[9], (2, HEADS), ((0, 2), (1, 2)), -0.2, 0.2), -7.0, -5.0),
        "decay_log": jnp.clip(-2.0 + 5.0 * jax.random.uniform(splits[10], (2, HEADS), jnp.float32) ** block_levels(splits[10], (2, HEADS), ((0, 2), (1, 2)), -0.2, 0.2), -2.0, 3.0),
        "skip_gain": jnp.clip(0.5 + 1.0 * jax.random.uniform(splits[11], (2, HEADS), jnp.float32) ** block_levels(splits[11], (2, HEADS), ((0, 2), (1, 2)), -0.2, 0.2), 0.5, 1.5),
        "gate_gain": jnp.clip(1.0 + 0.1 * jax.random.normal(splits[12], (2, E), jnp.float32), 0.5, 1.5),
        "output_proj": bell_draw(splits[13], (2, D, E), E ** -0.5, 0.125, ((0, 2), (1, 2), (2, 2))),
    }


EPS = 1e-05
HIGH = lax.Precision.HIGHEST

def round_trip(values):
    narrow = lax.optimization_barrier(values.astype(jnp.bfloat16))
    return narrow.astype(jnp.float32)

def norm_apply(hidden, scale_vec):
    factor = lax.rsqrt(lax.optimization_barrier(jnp.mean(hidden * hidden, axis=-1, keepdims=True)) + EPS)
    return hidden * factor * scale_vec[None, :]

def conv_apply(padded, kernel, offsets, seg_pad):
    length = padded.shape[0] - (CONV - 1)
    current = seg_pad[CONV - 1:]
    total = jnp.zeros((length, padded.shape[1]), jnp.float32) + offsets[None, :]
    for lag in range(CONV):
        same = (seg_pad[lag:lag + length] == current).astype(jnp.float32)
        total = total + kernel[lag][None, :] * padded[lag:lag + length] * same[:, None]
    return jax.nn.silu(total)

def gate_apply(ssd_flat, gate_vals, scale_vec):
    gated = ssd_flat * jax.nn.silu(gate_vals)
    return (gated * scale_vec[None, :], lax.optimization_barrier(jnp.sum(gated * gated, axis=1)))

def ssd_apply(x_heads, b_rows, c_rows, dt_raw, step_vec, log_vec, skip_vec, state_in, segs, seg_before):
    tokens = x_heads.shape[0]
    heads = x_heads.shape[1]
    blocks = tokens // SPAN
    delta = jax.nn.softplus(dt_raw + step_vec[None, :])
    rates = -jnp.exp(log_vec)[None, :] * delta
    x_blocks = x_heads.reshape(blocks, SPAN, heads, HEAD_DIM)
    b_blocks = b_rows.reshape(blocks, SPAN, STATE)
    c_blocks = c_rows.reshape(blocks, SPAN, STATE)
    delta_blocks = delta.reshape(blocks, SPAN, heads)
    cumul = jnp.cumsum(rates.reshape(blocks, SPAN, heads), axis=1)
    seg_blocks = segs.reshape(blocks, SPAN).astype(jnp.int32)
    seg_prior = jnp.concatenate([jnp.reshape(seg_before, (1,)).astype(jnp.int32), seg_blocks[:-1, -1]])
    positions = jnp.arange(SPAN)
    causal = positions[:, None] >= positions[None, :]
    mask = causal[None, :, :] & (seg_blocks[:, :, None] == seg_blocks[:, None, :])
    mask_heads = mask[..., None]
    spread = cumul[:, :, None, :] - cumul[:, None, :, :]
    decays = jnp.where(mask_heads, jnp.exp(jnp.where(mask_heads, spread, 0.0)), 0.0)
    scores = jnp.einsum('ktn,ksn->kts', c_blocks, b_blocks, precision=HIGH)
    mixing = scores[..., None] * decays * delta_blocks[:, None, :, :]
    inside = jnp.einsum('ktsh,kshp->kthp', mixing, x_blocks, precision=HIGH)
    last_same = (seg_blocks == seg_blocks[:, -1:])[..., None]
    tails = jnp.where(last_same, jnp.exp(cumul[:, -1:, :] - cumul), 0.0) * delta_blocks
    block_states = jnp.einsum('ksh,kshp,ksn->khpn', tails, x_blocks, b_blocks, precision=HIGH)
    keeps = (seg_blocks[:, -1] == seg_prior).astype(jnp.float32)
    block_decay = jnp.exp(cumul[:, -1, :]) * keeps[:, None]
    entry = jnp.exp(cumul) * (seg_blocks == seg_prior[:, None]).astype(jnp.float32)[..., None]

    def advance(state, items):
        entry_block, c_block, decay_block, state_block = items
        reads = jnp.einsum('tn,hpn->thp', c_block, state, precision=HIGH)
        return (decay_block[:, None, None] * state + state_block, entry_block[:, :, None] * reads)
    final_state, carried = lax.scan(advance, state_in, (entry, c_blocks, block_decay, block_states))
    result = (inside + carried).reshape(tokens, heads, HEAD_DIM) + skip_vec[None, :, None] * x_heads
    return (result, final_state)

def split_mixed(mixed, tokens):
    x_heads = mixed[:, :E].reshape(tokens, HEADS, HEAD_DIM)
    return (x_heads, mixed[:, E:E + STATE], mixed[:, E + STATE:])

def layer_forward(hidden, segs, params):
    norm_scale, inner_weight, state_weight, kernel_inner, offset_inner, kernel_state, offset_state, step_vec, log_vec, skip_vec, gate_scale, output_weight = params
    tokens = hidden.shape[0]
    normed = norm_apply(hidden, norm_scale).astype(jnp.bfloat16)
    inner_all = jnp.dot(normed, inner_weight.reshape(D, 2 * E), preferred_element_type=jnp.float32).astype(jnp.bfloat16)
    state_all = jnp.dot(normed, state_weight, preferred_element_type=jnp.float32)
    conv_input = jnp.concatenate([inner_all[:, E:], state_all[:, :2 * STATE].astype(jnp.bfloat16)], axis=1)
    padded = jnp.concatenate([jnp.zeros((CONV - 1, E + 2 * STATE), jnp.bfloat16), conv_input], axis=0)
    seg_pad = jnp.concatenate([jnp.full((CONV - 1,), -1, jnp.int32), segs.astype(jnp.int32)])
    kernel = jnp.concatenate([kernel_inner, kernel_state], axis=1)
    offsets = jnp.concatenate([offset_inner, offset_state])
    mixed = round_trip(conv_apply(padded.astype(jnp.float32), kernel, offsets, seg_pad))
    x_heads, b_rows, c_rows = split_mixed(mixed, tokens)
    dt_raw = state_all[:, 2 * STATE:]
    zero_state = jnp.zeros((HEADS, HEAD_DIM, STATE), jnp.float32)
    ssd_out, _ = ssd_apply(x_heads, b_rows, c_rows, dt_raw, step_vec, log_vec, skip_vec, zero_state, segs, jnp.int32(-1))
    vpre, squares = gate_apply(ssd_out.reshape(tokens, E), inner_all[:, :E].astype(jnp.float32), gate_scale)
    vproj = vpre.astype(jnp.bfloat16)
    proj = lax.dot_general(vproj, output_weight, (((1,), (1,)), ((), ())), preferred_element_type=jnp.float32)
    rstd = lax.rsqrt(squares / E + EPS)
    return (hidden + rstd[:, None] * proj, (hidden, normed, inner_all, padded, dt_raw, vproj, proj, rstd))

def layer_backward(grad_out, saved, segs, params):
    norm_scale, inner_weight, state_weight, kernel_inner, offset_inner, kernel_state, offset_state, step_vec, log_vec, skip_vec, gate_scale, output_weight = params
    hidden, normed, inner_all, padded, dt_raw, vproj, proj, rstd = saved
    tokens = hidden.shape[0]
    dproj = (rstd[:, None] * grad_out).astype(jnp.bfloat16)
    drstd = lax.optimization_barrier(jnp.sum(grad_out * proj, axis=1))
    dvpre = jnp.dot(dproj, output_weight, preferred_element_type=jnp.float32)
    dsquares = -0.5 * drstd * rstd * rstd * rstd / E
    seg_pad = jnp.concatenate([jnp.full((CONV - 1,), -1, jnp.int32), segs.astype(jnp.int32)])
    kernel = jnp.concatenate([kernel_inner, kernel_state], axis=1)
    offsets = jnp.concatenate([offset_inner, offset_state])

    def conv_local(rows, kernel_all, offset_all):
        return conv_apply(rows, kernel_all, offset_all, seg_pad)
    mixed_raw, conv_pull = jax.vjp(conv_local, padded.astype(jnp.float32), kernel, offsets)
    x_heads, b_rows, c_rows = split_mixed(round_trip(mixed_raw), tokens)
    zero_state = jnp.zeros((HEADS, HEAD_DIM, STATE), jnp.float32)

    def ssd_local(x_in, b_in, c_in, raw_in, step_in, log_in, skip_in, state_start):
        return ssd_apply(x_in, b_in, c_in, raw_in, step_in, log_in, skip_in, state_start, segs, jnp.int32(-1))
    (ssd_out, _), ssd_pull = jax.vjp(ssd_local, x_heads, b_rows, c_rows, dt_raw, step_vec, log_vec, skip_vec, zero_state)
    _, gate_pull = jax.vjp(gate_apply, ssd_out.reshape(tokens, E), inner_all[:, :E].astype(jnp.float32), gate_scale)
    dssd, dgate_in, dgate_scale = gate_pull((dvpre, dsquares))
    dx_heads, db_rows, dc_rows, ddt_raw, dstep, ddecay, dskip, _ = ssd_pull((dssd.reshape(tokens, HEADS, HEAD_DIM), zero_state))
    dmixed = jnp.concatenate([dx_heads.reshape(tokens, E), db_rows, dc_rows], axis=1)
    dpadded, dkernel, doffsets = conv_pull(dmixed)
    dconv = dpadded[CONV - 1:]
    dinner = jnp.concatenate([dgate_in, dconv[:, :E]], axis=1).astype(jnp.bfloat16)
    dstate = jnp.concatenate([dconv[:, E:], ddt_raw], axis=1).astype(jnp.bfloat16)
    contract_cols = (((1,), (1,)), ((), ()))
    contract_rows = (((0,), (0,)), ((), ()))
    dnormed = lax.dot_general(dinner, inner_weight.reshape(D, 2 * E), contract_cols, preferred_element_type=jnp.float32)
    dnormed = dnormed + lax.dot_general(dstate, state_weight, contract_cols, preferred_element_type=jnp.float32)
    _, norm_pull = jax.vjp(norm_apply, hidden, norm_scale)
    dhidden, dnorm_scale = norm_pull(dnormed)
    grads = (dnorm_scale, lax.dot_general(normed, dinner, contract_rows, preferred_element_type=jnp.float32).reshape(D, 2, E), lax.dot_general(normed, dstate, contract_rows, preferred_element_type=jnp.float32), dkernel[:, :E], doffsets[:E], dkernel[:, E:], doffsets[E:], dstep, ddecay, dskip, dgate_scale, lax.dot_general(dproj, vproj, contract_rows, preferred_element_type=jnp.float32))
    return (grad_out + dhidden, grads)

def reference(boundary, segments, norm_gain, inner_proj, state_proj, conv_inner, conv_inner_bias, conv_state, conv_state_bias, step_bias, decay_log, skip_gain, gate_gain, output_proj):
    stacked = (norm_gain, inner_proj, state_proj, conv_inner, conv_inner_bias, conv_state, conv_state_bias, step_bias, decay_log, skip_gain, gate_gain, output_proj)
    first = tuple((item[0] for item in stacked))
    second = tuple((item[1] for item in stacked))

    def accumulate(total, first_grad, second_grad):
        return total + jnp.stack([first_grad, second_grad])

    def per_sequence(totals, items):
        block_in, cotangent, segs = items
        middle, saved_first = layer_forward(block_in, segs, first)
        top, saved_second = layer_forward(middle, segs, second)
        dmiddle, grads_second = layer_backward(cotangent, saved_second, segs, second)
        dinput, grads_first = layer_backward(dmiddle, saved_first, segs, first)
        totals = jax.tree.map(accumulate, totals, grads_first, grads_second)
        return (totals, (dinput, top))
    initial = tuple((jnp.zeros(item.shape, jnp.float32) for item in stacked))
    totals, (dinputs, tops) = lax.scan(per_sequence, initial, (boundary[0], boundary[1], segments))
    return (jnp.stack([dinputs, tops]), totals[0], totals[1], totals[2], totals[3], totals[4], totals[5], totals[6], totals[7], totals[8], totals[9], totals[10], totals[11])
```

```python
import jax
import jax.numpy as jnp
from jax import lax
from jax.sharding import PartitionSpec as P

HEAD_DIM = 64
CONV = 4
LONGEST = 512
EPS = 1e-05
BF16 = jnp.bfloat16
F32 = jnp.float32
ROWS = (((0,), (0,)), ((), ()))
COLS = (((1,), (1,)), ((), ()))


def send(value, axis, shift, layer, wrap=False):
    count = lax.axis_size(axis)
    base = layer * count
    pairs = [
        (base + place, base + (place + shift) % count)
        for place in range(count)
        if wrap or 0 <= place + shift < count
    ]
    return lax.ppermute(value, ("section", axis), pairs)


def hand_over(value, steps):
    count = lax.axis_size("section")
    leading, last = (max(0, -steps), min(count, count - steps))
    return lax.ppermute(value, "section", [(place, place + steps) for place in range(leading, last)])


def tp_sum(value, layer):
    if lax.axis_size("tp") == 2:
        value = lax.optimization_barrier(value)
        return value.astype(F32) + send(value, "tp", 1, layer, True).astype(F32)
    return jnp.sum(lax.all_gather(value, "tp").astype(F32), axis=0)


def carried_in(decay, state, direction, layer):
    tokens = state[1]
    state = state[0]
    heads, _, width = state.shape
    reach = min(lax.axis_size("ctx") - 1, -(-(LONGEST - 1) // tokens))
    packed = jnp.concatenate(
        [state, jnp.broadcast_to(decay[:, None, None], (heads, 8, width))], axis=1
    ).astype(BF16)
    parts = [send(packed, "ctx", direction * (hop + 1), layer).astype(F32) for hop in range(reach)]
    total = jnp.zeros_like(state)
    for part in reversed(parts):
        total = part[:, :HEAD_DIM] + part[:, HEAD_DIM : HEAD_DIM + 1, :1] * total
    return total


def round_trip(values):
    narrow = lax.optimization_barrier(values.astype(BF16))
    return narrow.astype(F32)


def norm_apply(hidden, scale_vec):
    factor = lax.rsqrt(jnp.mean(hidden * hidden, axis=-1, keepdims=True) + EPS)
    return hidden * factor * scale_vec[None, :]


def conv_apply(padded, kernel, offsets, seg_pad):
    length = padded.shape[0] - (CONV - 1)
    current = seg_pad[CONV - 1 :]
    total = jnp.zeros((length, padded.shape[1]), F32) + offsets[None, :]
    for lag in range(CONV):
        same = (seg_pad[lag : lag + length] == current).astype(F32)
        total = total + kernel[lag][None, :] * padded[lag : lag + length] * same[:, None]
    return jax.nn.silu(total)


def gate_apply(ssd_flat, gate_vals, scale_vec):
    gated = ssd_flat * jax.nn.silu(gate_vals)
    return (gated * scale_vec[None, :], jnp.sum(gated * gated, axis=1))


def step_terms(dt_raw, step_vec, log_vec):
    tokens = dt_raw.shape[1]
    delta = jax.nn.softplus(dt_raw + step_vec[:, None])
    rates = -jnp.exp(log_vec)[:, None] * delta
    places = jnp.arange(tokens)
    upto = (places[:, None] <= places[None, :]).astype(F32)
    return delta, jnp.dot(rates, upto, precision=lax.Precision.HIGHEST)


def local_state(x_heads, b_rows, delta, cumul, segs):
    last_same = (segs == segs[-1])[None, :]
    tails = jnp.where(last_same, jnp.exp(cumul[:, -1:] - cumul), 0.0) * delta
    return jnp.einsum("hsp,sn->hpn", tails[:, :, None] * x_heads, b_rows)


def entries(cumul, segs, seg_before):
    return jnp.exp(cumul) * (segs == seg_before).astype(F32)[None, :]


def ssd_apply(
    x_heads, b_rows, c_rows, dt_raw, step_vec, log_vec, skip_vec, state_in, segs, seg_before
):
    tokens = x_heads.shape[1]
    delta, cumul = step_terms(dt_raw, step_vec, log_vec)
    places = jnp.arange(tokens)
    mask = ((places[:, None] >= places[None, :]) & (segs[:, None] == segs[None, :]))[None]
    spread = cumul[:, :, None] - cumul[:, None, :]
    decays = jnp.where(mask, jnp.exp(jnp.where(mask, spread, 0.0)), 0.0)
    scores = jnp.einsum("tn,sn->ts", c_rows, b_rows)
    mixing = scores[None] * decays * delta[:, None, :]
    inside = jnp.einsum("hts,hsp->htp", mixing, x_heads)
    reads = jnp.einsum("tn,hpn->htp", c_rows, state_in)
    carried = entries(cumul, segs, seg_before)[:, :, None] * reads
    result = inside + carried + skip_vec[:, None, None] * x_heads
    keeps = (segs[-1] == seg_before).astype(F32)
    block_decay = jnp.exp(cumul[:, -1]) * keeps
    final = block_decay[:, None, None] * state_in + local_state(
        x_heads, b_rows, delta, cumul, segs
    )
    return (result, final)


def owned_grad(left, right, layer):
    shards = lax.axis_size("shard")
    count = lax.axis_size("ctx")
    place = lax.axis_index("ctx")
    block = left.shape[1] // shards

    def part(index):
        return lax.dot_general(
            left[:, index * block : (index + 1) * block], right, ROWS, preferred_element_type=F32
        )

    away = [send(part(k).astype(BF16), "shard", k, layer, True) for k in range(1, shards)]
    total = part(0)
    for value in away:
        total = total + value.astype(F32)
    rows = block // count
    narrow = total.astype(BF16)
    result = lax.dynamic_slice_in_dim(total, place * rows, rows, 0)
    for k in range(1, count):
        piece = lax.dynamic_slice_in_dim(narrow, lax.rem(place + k, count) * rows, rows, 0)
        result = result + send(piece, "ctx", k, layer, True).astype(F32)
    return result


def place_cols(values, full_width, start, axis_pos):
    shape_full = values.shape[:axis_pos] + (full_width,) + values.shape[axis_pos + 1 :]
    return lax.dynamic_update_slice_in_dim(jnp.zeros(shape_full, F32), values, start, axis_pos)


def turned(values, start, axis_pos):
    return lax.dynamic_slice_in_dim(
        jnp.concatenate([values, values], axis=axis_pos), start, values.shape[axis_pos], axis_pos
    )


def per_device(
    boundary,
    segments,
    norm_gain,
    inner_proj,
    state_proj,
    conv_inner,
    conv_inner_bias,
    conv_state,
    conv_state_bias,
    step_bias,
    decay_log,
    skip_gain,
    gate_gain,
    output_proj,
):
    section_pos = lax.axis_index("section")
    shard_pos = lax.axis_index("shard")
    shard_count = lax.axis_size("shard")
    ctx_pos = lax.axis_index("ctx")
    tp_pos = lax.axis_index("tp")
    tp_count = lax.axis_size("tp")
    tokens, width = boundary.shape[2:]
    rows = inner_proj.shape[1]
    heads_local = step_bias.shape[1]
    inner_local = conv_inner.shape[2]
    state_size = conv_state.shape[2] // 2
    heads_total = heads_local * tp_count
    inner_total = inner_local * tp_count
    turn = shard_pos * rows
    stream = turned(boundary[0, 0], turn, 1)
    norm_scale = turned(norm_gain[0], turn, 0)
    seq_all = segments[0]
    seg_pad = jnp.concatenate([jnp.full((CONV - 1,), -1, jnp.int32), seq_all])
    first_token = ctx_pos * tokens
    seg_ext = lax.dynamic_slice_in_dim(seg_pad, first_token, tokens + CONV - 1)
    seg_local = lax.dynamic_slice_in_dim(seq_all, first_token, tokens)
    seg_before = seg_ext[CONV - 2]
    keeps = (seg_local[-1] == seg_before).astype(F32)
    own_weights = (
        inner_proj[0].reshape(rows, 2 * inner_local),
        state_proj[0],
        output_proj[0],
    )
    kernel = jnp.concatenate([conv_inner[0], conv_state[0]], axis=1)
    offsets = jnp.concatenate([conv_inner_bias[0], conv_state_bias[0]])
    step_vec = step_bias[0]
    log_vec = decay_log[0]
    skip_vec = skip_gain[0]
    gate_scale = gate_gain[0]

    def fetch(weights, layer):
        return [
            [own] + [send(value, "shard", -k, layer, True) for k in range(1, shard_count)]
            for own, value in zip(own_weights, weights)
        ]

    def by_rows(values, weight):
        total = None
        for k, part in enumerate(weight):
            product = jnp.dot(
                values[:, k * rows : (k + 1) * rows], part, preferred_element_type=F32
            )
            total = product if total is None else total + product
        return total

    def to_rows(values, weight):
        return jnp.concatenate(
            [lax.dot_general(values, part, COLS, preferred_element_type=F32) for part in weight],
            axis=1,
        )

    def split_mixed(mixed):
        x_heads = mixed[:, :inner_local].reshape(tokens, heads_local, HEAD_DIM)
        return (
            jnp.swapaxes(x_heads, 0, 1),
            mixed[:, inner_local : inner_local + state_size],
            mixed[:, inner_local + state_size :],
        )

    def flat_heads(values):
        return jnp.swapaxes(values, 0, 1).reshape(tokens, inner_local)

    def head_rows(values):
        return jnp.swapaxes(values.reshape(tokens, heads_local, HEAD_DIM), 0, 1)

    def ssd_local(x_in, b_in, c_in, raw_in, step_in, log_in, skip_in, state_start):
        return ssd_apply(
            x_in, b_in, c_in, raw_in, step_in, log_in, skip_in, state_start, seg_local, seg_before
        )

    def conv_local(values, kernel_all, offset_all):
        return conv_apply(values, kernel_all, offset_all, seg_ext)

    def forward(stream_in, weights, layer):
        inner_weight, state_weight, output_weight = weights
        normed = norm_apply(stream_in, norm_scale).astype(BF16)
        inner_all = by_rows(normed, inner_weight).astype(BF16)
        state_all = by_rows(normed, state_weight)
        dt_raw = lax.dynamic_slice_in_dim(
            state_all, 2 * state_size + tp_pos * heads_local, heads_local, 1
        ).T
        conv_input = jnp.concatenate(
            [inner_all[:, inner_local:], state_all[:, : 2 * state_size].astype(BF16)], axis=1
        )
        previous = send(conv_input[tokens - (CONV - 1) :], "ctx", 1, layer)
        padded = jnp.concatenate([previous, conv_input], axis=0)
        mixed = round_trip(conv_apply(padded.astype(F32), kernel, offsets, seg_ext))
        x_heads, b_rows, c_rows = split_mixed(mixed)
        delta, cumul = step_terms(dt_raw, step_vec, log_vec)
        decay = jnp.exp(cumul[:, -1]) * keeps
        state = local_state(x_heads, b_rows, delta, cumul, seg_local)
        state_in = carried_in(decay, (state, tokens), 1, layer)
        ssd_out, _ = ssd_local(
            x_heads, b_rows, c_rows, dt_raw, step_vec, log_vec, skip_vec, state_in
        )
        vpre, squares = gate_apply(
            flat_heads(ssd_out), inner_all[:, :inner_local].astype(F32), gate_scale
        )
        vproj = vpre.astype(BF16)
        squares_sum = tp_sum(squares, layer)
        proj = tp_sum(to_rows(vproj, output_weight).astype(BF16), layer)
        rstd = lax.rsqrt(squares_sum / inner_total + EPS)
        output = stream_in + rstd[:, None] * proj
        return (
            output,
            (stream_in, normed, inner_all, padded, dt_raw, state_in, decay, vproj, proj, rstd),
        )

    def backward(grad_out, saved, weights, layer):
        inner_weight, state_weight, output_weight = weights
        stream_in, normed, inner_all, padded, dt_raw, state_in, decay, vproj, proj, rstd = saved
        dproj = (rstd[:, None] * grad_out).astype(BF16)
        grad_output = owned_grad(dproj, vproj, layer)
        drstd = jnp.sum(grad_out * proj, axis=1)
        dvpre = by_rows(dproj, output_weight)
        dsquares = -0.5 * drstd * rstd * rstd * rstd / inner_total
        mixed_raw, conv_pull = jax.vjp(conv_local, padded.astype(F32), kernel, offsets)
        x_heads, b_rows, c_rows = split_mixed(round_trip(mixed_raw))
        (ssd_out, _), ssd_pull = jax.vjp(
            ssd_local, x_heads, b_rows, c_rows, dt_raw, step_vec, log_vec, skip_vec, state_in
        )
        _, gate_pull = jax.vjp(
            gate_apply, flat_heads(ssd_out), inner_all[:, :inner_local].astype(F32), gate_scale
        )
        dssd, dgate_in, dgate_scale = gate_pull((dvpre, dsquares))
        dgate = dgate_in.astype(BF16)
        grad_gate = owned_grad(normed, dgate, layer)
        dssd_heads = head_rows(dssd)
        _, cumul = step_terms(dt_raw, step_vec, log_vec)
        entry = entries(cumul, seg_local, seg_before)
        local_grad = jnp.einsum("tn,htp->hpn", c_rows, entry[:, :, None] * dssd_heads)
        state_grad = carried_in(decay, (local_grad, tokens), -1, layer)
        dx_heads, db_rows, dc_rows, ddt_raw, dstep, ddecay, dskip, _ = ssd_pull(
            (dssd_heads, state_grad)
        )
        dmixed = jnp.concatenate([flat_heads(dx_heads), db_rows, dc_rows], axis=1)
        dpadded, dkernel, doffsets = conv_pull(dmixed)
        spill = send(dpadded[: CONV - 1], "ctx", -1, layer)
        dconv = dpadded[CONV - 1 :] + jnp.pad(spill, ((tokens - (CONV - 1), 0), (0, 0)))
        dmix = dconv[:, :inner_local].astype(BF16)
        grad_mix = owned_grad(normed, dmix, layer)
        ddt_full = place_cols(ddt_raw.T, heads_total, tp_pos * heads_local, 1)
        dstate_part = jnp.concatenate([dconv[:, inner_local:], ddt_full], axis=1)
        dinner = jnp.concatenate([dgate, dmix], axis=1)
        dnormed_part = to_rows(dinner, inner_weight)
        dstate = tp_sum(dstate_part.astype(BF16), layer).astype(BF16)
        grad_state = owned_grad(normed, dstate, layer)
        dnormed = tp_sum(dnormed_part.astype(BF16), layer) + to_rows(dstate, state_weight)
        _, norm_pull = jax.vjp(norm_apply, stream_in, norm_scale)
        dstream, dnorm_scale = norm_pull(dnormed)
        tp_first = (tp_pos == 0).astype(F32)
        smalls = (
            turned(dnorm_scale, width - turn, 0) * tp_first,
            place_cols(dkernel[:, :inner_local], inner_total, tp_pos * inner_local, 1),
            place_cols(doffsets[:inner_local], inner_total, tp_pos * inner_local, 0),
            dkernel[:, inner_local:],
            doffsets[inner_local:],
            place_cols(dstep, heads_total, tp_pos * heads_local, 0),
            place_cols(ddecay, heads_total, tp_pos * heads_local, 0),
            place_cols(dskip, heads_total, tp_pos * heads_local, 0),
            place_cols(dgate_scale, inner_total, tp_pos * inner_local, 0),
        )
        return (grad_out + dstream, (grad_gate, grad_mix, grad_state, grad_output), smalls)

    section_zero = section_pos == 0

    def pick_zero(from_zero, from_one):
        return jnp.where(section_zero, from_zero, from_one)

    weights_zero = fetch(own_weights, 0)
    out_first, saved_first = forward(stream, weights_zero, 0)
    later, _ = lax.optimization_barrier((own_weights, saved_first[2]))
    weights_one = fetch(later, 1)
    received = hand_over(out_first, 1)
    out_second, saved_second = forward(received, weights_one, 1)
    saved = jax.tree.map(pick_zero, saved_first, saved_second)
    cot_first = jnp.where(section_zero, jnp.zeros_like(stream), stream)
    grad_first, mats_first, small_first = backward(cot_first, saved, weights_one, 1)
    returned = hand_over(grad_first.astype(BF16), -1).astype(F32)
    grad_second, mats_second, small_second = backward(returned, saved, weights_zero, 0)
    grad_gate, grad_mix, grad_state, grad_output = jax.tree.map(pick_zero, mats_second, mats_first)
    smalls = jax.tree.map(pick_zero, small_second, small_first)
    boundary_out = turned(jnp.where(section_zero, grad_second, out_second), width - turn, 1)
    flat = jnp.concatenate([value.reshape(-1) for value in smalls])
    flat = jnp.pad(flat, (0, -flat.shape[0] % 1024)).reshape(-1, 128)
    flat = lax.psum(flat, ("shard", "ctx", "tp")).reshape(-1)
    sums, start = [], 0
    for value in smalls:
        sums.append(flat[start : start + value.size].reshape((1,) + value.shape))
        start += value.size
    return (
        boundary_out[None, None],
        sums[0],
        jnp.stack([grad_gate, grad_mix], axis=1)[None],
        grad_state[None],
        *sums[1:],
        grad_output[None],
    )


def solution(mesh):
    in_specs = (
        P("section", "shard", "ctx", None),
        P("shard", None),
        P("section", None),
        P("section", "shard", None, "tp"),
        P("section", "shard", None),
        P("section", None, "tp"),
        P("section", "tp"),
        P("section", None, None),
        P("section", None),
        P("section", "tp"),
        P("section", "tp"),
        P("section", "tp"),
        P("section", "tp"),
        P("section", "shard", "tp"),
    )
    out_specs = (
        P("section", "shard", "ctx", None),
        P("section", None),
        P("section", ("shard", "ctx"), None, "tp"),
        P("section", ("shard", "ctx"), None),
        P("section", None, None),
        P("section", None),
        P("section", None, None),
        P("section", None),
        P("section", None),
        P("section", None),
        P("section", None),
        P("section", None),
        P("section", ("shard", "ctx"), "tp"),
    )
    return jax.shard_map(
        per_device, mesh=mesh, in_specs=in_specs, out_specs=out_specs, check_vma=False
    )
```

```python
import jax
import jax.numpy as jnp
from jax import lax
from jax.sharding import PartitionSpec as P

HEAD_DIM = 64
CONV = 4
LONGEST = 512
EPS = 1e-05
BF16 = jnp.bfloat16
F32 = jnp.float32
ROWS = (((0,), (0,)), ((), ()))
COLS = (((1,), (1,)), ((), ()))


def send(value, axis, shift, layer, wrap=False):
    count = lax.axis_size(axis)
    base = layer * count
    pairs = [
        (base + place, base + (place + shift) % count)
        for place in range(count)
        if wrap or 0 <= place + shift < count
    ]
    return lax.ppermute(value, ("section", axis), pairs)


def hand_over(value, steps):
    count = lax.axis_size("section")
    leading, last = (max(0, -steps), min(count, count - steps))
    return lax.ppermute(value, "section", [(place, place + steps) for place in range(leading, last)])


def tp_sum(value, layer):
    if lax.axis_size("tp") == 2:
        value = lax.optimization_barrier(value)
        return value.astype(F32) + send(value, "tp", 1, layer, True).astype(F32)
    return jnp.sum(lax.all_gather(value, "tp").astype(F32), axis=0)


def carried_in(decay, state, direction, layer):
    tokens = state[1]
    state = state[0]
    heads, _, width = state.shape
    reach = min(lax.axis_size("ctx") - 1, -(-(LONGEST - 1) // tokens))
    packed = jnp.concatenate(
        [state, jnp.broadcast_to(decay[:, None, None], (heads, 8, width))], axis=1
    ).astype(BF16)
    parts = [send(packed, "ctx", direction * (hop + 1), layer).astype(F32) for hop in range(reach)]
    total = jnp.zeros_like(state)
    for part in reversed(parts):
        total = part[:, :HEAD_DIM] + part[:, HEAD_DIM : HEAD_DIM + 1, :1] * total
    return total


def round_trip(values):
    narrow = lax.optimization_barrier(values.astype(BF16))
    return narrow.astype(F32)


def norm_apply(hidden, scale_vec):
    factor = lax.rsqrt(jnp.mean(hidden * hidden, axis=-1, keepdims=True) + EPS)
    return hidden * factor * scale_vec[None, :]


def conv_apply(padded, kernel, offsets, seg_pad):
    length = padded.shape[0] - (CONV - 1)
    current = seg_pad[CONV - 1 :]
    total = jnp.zeros((length, padded.shape[1]), F32) + offsets[None, :]
    for lag in range(CONV):
        same = (seg_pad[lag : lag + length] == current).astype(F32)
        total = total + kernel[lag][None, :] * padded[lag : lag + length] * same[:, None]
    return jax.nn.silu(total)


def gate_apply(ssd_flat, gate_vals, scale_vec):
    gated = ssd_flat * jax.nn.silu(gate_vals)
    return (gated * scale_vec[None, :], jnp.sum(gated * gated, axis=1))


def step_terms(dt_raw, step_vec, log_vec):
    tokens = dt_raw.shape[1]
    delta = jax.nn.softplus(dt_raw + step_vec[:, None])
    rates = -jnp.exp(log_vec)[:, None] * delta
    places = jnp.arange(tokens)
    upto = (places[:, None] <= places[None, :]).astype(F32)
    return delta, jnp.dot(rates, upto, precision=lax.Precision.HIGHEST)


def local_state(x_heads, b_rows, delta, cumul, segs):
    last_same = (segs == segs[-1])[None, :]
    tails = jnp.where(last_same, jnp.exp(cumul[:, -1:] - cumul), 0.0) * delta
    return jnp.einsum("hsp,sn->hpn", tails[:, :, None] * x_heads, b_rows)


def entries(cumul, segs, seg_before):
    return jnp.exp(cumul) * (segs == seg_before).astype(F32)[None, :]


def ssd_apply(
    x_heads, b_rows, c_rows, dt_raw, step_vec, log_vec, skip_vec, state_in, segs, seg_before
):
    tokens = x_heads.shape[1]
    delta, cumul = step_terms(dt_raw, step_vec, log_vec)
    places = jnp.arange(tokens)
    mask = ((places[:, None] >= places[None, :]) & (segs[:, None] == segs[None, :]))[None]
    spread = cumul[:, :, None] - cumul[:, None, :]
    decays = jnp.where(mask, jnp.exp(jnp.where(mask, spread, 0.0)), 0.0)
    scores = jnp.einsum("tn,sn->ts", c_rows, b_rows)
    mixing = scores[None] * decays * delta[:, None, :]
    inside = jnp.einsum("hts,hsp->htp", mixing, x_heads)
    reads = jnp.einsum("tn,hpn->htp", c_rows, state_in)
    carried = entries(cumul, segs, seg_before)[:, :, None] * reads
    result = inside + carried + skip_vec[:, None, None] * x_heads
    keeps = (segs[-1] == seg_before).astype(F32)
    block_decay = jnp.exp(cumul[:, -1]) * keeps
    final = block_decay[:, None, None] * state_in + local_state(
        x_heads, b_rows, delta, cumul, segs
    )
    return (result, final)


def cross_grad(pairs, layer):
    shards = lax.axis_size("shard")

    def part(index, kind):
        products = []
        for left, right in pairs:
            block = left.shape[1] // shards
            taken = left[:, index * block : (index + 1) * block]
            products.append(
                lax.dot_general(taken, right, ROWS, preferred_element_type=F32).astype(kind)
            )
        return jnp.concatenate(products, axis=1)

    away = [send(part(k, BF16), "shard", k, layer, True) for k in range(1, shards)]
    total = part(0, F32)
    for value in away:
        total = total + value.astype(F32)
    return total


def even_pairs(axis, distance, layer):
    count = lax.axis_size(axis)
    return [(layer * count + place, layer * count + (place ^ distance)) for place in range(count)]


def own_rows(total, layer):
    count = lax.axis_size("ctx")
    place = lax.axis_index("ctx")
    blocks = total.reshape(count, total.shape[0] // count, total.shape[1])
    if count & (count - 1):
        blocks = lax.psum_scatter(blocks.astype(BF16), "ctx", scatter_dimension=0, tiled=True)
        return blocks[0].astype(F32)
    distance = 1
    while distance < count:
        bit = lax.rem(place // distance, 2)
        pairs = blocks.reshape((blocks.shape[0] // 2, 2) + blocks.shape[1:])
        mine = lax.dynamic_index_in_dim(pairs, bit, 1, False)
        theirs = lax.dynamic_index_in_dim(pairs, 1 - bit, 1, False).astype(BF16)
        got = lax.ppermute(theirs, ("section", "ctx"), even_pairs("ctx", distance, layer))
        blocks = mine + got.astype(F32)
        distance *= 2
    return blocks[0]


def all_sum(value):
    for axis in ("shard", "ctx", "tp"):
        count = lax.axis_size(axis)
        if count & (count - 1):
            value = lax.psum(value, axis)
            continue
        distance = 1
        while distance < count:
            pairs = [(place, place ^ distance) for place in range(count)]
            value = value + lax.ppermute(value, axis, pairs)
            distance *= 2
    return value


def place_cols(values, full_width, start, axis_pos):
    shape_full = values.shape[:axis_pos] + (full_width,) + values.shape[axis_pos + 1 :]
    return lax.dynamic_update_slice_in_dim(jnp.zeros(shape_full, F32), values, start, axis_pos)


def turned(values, start, axis_pos):
    return lax.dynamic_slice_in_dim(
        jnp.concatenate([values, values], axis=axis_pos), start, values.shape[axis_pos], axis_pos
    )


def per_device(
    boundary,
    segments,
    norm_gain,
    inner_proj,
    state_proj,
    conv_inner,
    conv_inner_bias,
    conv_state,
    conv_state_bias,
    step_bias,
    decay_log,
    skip_gain,
    gate_gain,
    output_proj,
):
    section_pos = lax.axis_index("section")
    shard_pos = lax.axis_index("shard")
    shard_count = lax.axis_size("shard")
    ctx_pos = lax.axis_index("ctx")
    tp_pos = lax.axis_index("tp")
    tp_count = lax.axis_size("tp")
    tokens, width = boundary.shape[2:]
    rows = inner_proj.shape[1]
    heads_local = step_bias.shape[1]
    inner_local = conv_inner.shape[2]
    state_size = conv_state.shape[2] // 2
    heads_total = heads_local * tp_count
    inner_total = inner_local * tp_count
    turn = shard_pos * rows
    stream = turned(boundary[0, 0], turn, 1)
    norm_scale = turned(norm_gain[0], turn, 0)
    seq_all = segments[0]
    seg_pad = jnp.concatenate([jnp.full((CONV - 1,), -1, jnp.int32), seq_all])
    first_token = ctx_pos * tokens
    seg_ext = lax.dynamic_slice_in_dim(seg_pad, first_token, tokens + CONV - 1)
    seg_local = lax.dynamic_slice_in_dim(seq_all, first_token, tokens)
    seg_before = seg_ext[CONV - 2]
    keeps = (seg_local[-1] == seg_before).astype(F32)
    own_input = jnp.concatenate(
        [inner_proj[0, :, 0], inner_proj[0, :, 1], state_proj[0]], axis=1
    )
    own_output = output_proj[0]
    kernel = jnp.concatenate([conv_inner[0], conv_state[0]], axis=1)
    offsets = jnp.concatenate([conv_inner_bias[0], conv_state_bias[0]])
    step_vec = step_bias[0]
    log_vec = decay_log[0]
    skip_vec = skip_gain[0]
    gate_scale = gate_gain[0]

    def fetch(own, after, layer):
        sent, _ = lax.optimization_barrier((own, after))
        return [own] + [send(sent, "shard", -k, layer, True) for k in range(1, shard_count)]

    def by_rows(values, weight):
        total = None
        for k, part in enumerate(weight):
            product = jnp.dot(
                values[:, k * rows : (k + 1) * rows], part, preferred_element_type=F32
            )
            total = product if total is None else total + product
        return total

    def to_rows(values, weight):
        return jnp.concatenate(
            [lax.dot_general(values, part, COLS, preferred_element_type=F32) for part in weight],
            axis=1,
        )

    def split_mixed(mixed):
        x_heads = mixed[:, :inner_local].reshape(tokens, heads_local, HEAD_DIM)
        return (
            jnp.swapaxes(x_heads, 0, 1),
            mixed[:, inner_local : inner_local + state_size],
            mixed[:, inner_local + state_size :],
        )

    def flat_heads(values):
        return jnp.swapaxes(values, 0, 1).reshape(tokens, inner_local)

    def head_rows(values):
        return jnp.swapaxes(values.reshape(tokens, heads_local, HEAD_DIM), 0, 1)

    def ssd_local(x_in, b_in, c_in, raw_in, step_in, log_in, skip_in, state_start):
        return ssd_apply(
            x_in, b_in, c_in, raw_in, step_in, log_in, skip_in, state_start, seg_local, seg_before
        )

    def conv_local(values, kernel_all, offset_all):
        return conv_apply(values, kernel_all, offset_all, seg_ext)

    def forward(stream_in, weights, layer):
        input_weight, output_weight = weights
        normed = norm_apply(stream_in, norm_scale).astype(BF16)
        both = by_rows(normed, input_weight)
        inner_all = both[:, : 2 * inner_local].astype(BF16)
        state_all = both[:, 2 * inner_local :]
        dt_raw = lax.dynamic_slice_in_dim(
            state_all, 2 * state_size + tp_pos * heads_local, heads_local, 1
        ).T
        conv_input = jnp.concatenate(
            [inner_all[:, inner_local:], state_all[:, : 2 * state_size].astype(BF16)], axis=1
        )
        previous = send(conv_input[tokens - (CONV - 1) :], "ctx", 1, layer)
        padded = jnp.concatenate([previous, conv_input], axis=0)
        mixed = round_trip(conv_apply(padded.astype(F32), kernel, offsets, seg_ext))
        x_heads, b_rows, c_rows = split_mixed(mixed)
        delta, cumul = step_terms(dt_raw, step_vec, log_vec)
        decay = jnp.exp(cumul[:, -1]) * keeps
        state = local_state(x_heads, b_rows, delta, cumul, seg_local)
        state_in = carried_in(decay, (state, tokens), 1, layer)
        ssd_out, _ = ssd_local(
            x_heads, b_rows, c_rows, dt_raw, step_vec, log_vec, skip_vec, state_in
        )
        vpre, squares = gate_apply(
            flat_heads(ssd_out), inner_all[:, :inner_local].astype(F32), gate_scale
        )
        vproj = vpre.astype(BF16)
        high = lax.optimization_barrier(squares.astype(BF16))
        low = (squares - high.astype(F32)).astype(BF16)
        ends = jnp.pad(jnp.stack([high, low], axis=1), ((0, 0), (0, 126)))
        summed = tp_sum(
            jnp.concatenate([to_rows(vproj, output_weight).astype(BF16), ends], axis=1), layer
        )
        proj = summed[:, :width]
        squares_sum = summed[:, width] + summed[:, width + 1]
        rstd = lax.rsqrt(squares_sum / inner_total + EPS)
        output = stream_in + rstd[:, None] * proj
        return (
            output,
            (stream_in, normed, inner_all, padded, dt_raw, state_in, decay, vproj, proj, rstd),
        )

    def backward(grad_out, saved, weights, layer):
        input_weight, output_weight = weights
        stream_in, normed, inner_all, padded, dt_raw, state_in, decay, vproj, proj, rstd = saved
        dproj = (rstd[:, None] * grad_out).astype(BF16)
        drstd = jnp.sum(grad_out * proj, axis=1)
        dvpre = by_rows(dproj, output_weight)
        dsquares = -0.5 * drstd * rstd * rstd * rstd / inner_total
        mixed_raw, conv_pull = jax.vjp(conv_local, padded.astype(F32), kernel, offsets)
        x_heads, b_rows, c_rows = split_mixed(round_trip(mixed_raw))
        (ssd_out, _), ssd_pull = jax.vjp(
            ssd_local, x_heads, b_rows, c_rows, dt_raw, step_vec, log_vec, skip_vec, state_in
        )
        _, gate_pull = jax.vjp(
            gate_apply, flat_heads(ssd_out), inner_all[:, :inner_local].astype(F32), gate_scale
        )
        dssd, dgate_in, dgate_scale = gate_pull((dvpre, dsquares))
        dgate = dgate_in.astype(BF16)
        early = ((dproj, vproj), (normed, dgate))
        if layer == 0:
            early_sum = own_rows(cross_grad(early, layer), layer)
        dssd_heads = head_rows(dssd)
        _, cumul = step_terms(dt_raw, step_vec, log_vec)
        entry = entries(cumul, seg_local, seg_before)
        local_grad = jnp.einsum("tn,htp->hpn", c_rows, entry[:, :, None] * dssd_heads)
        state_grad = carried_in(decay, (local_grad, tokens), -1, layer)
        dx_heads, db_rows, dc_rows, ddt_raw, dstep, ddecay, dskip, _ = ssd_pull(
            (dssd_heads, state_grad)
        )
        dmixed = jnp.concatenate([flat_heads(dx_heads), db_rows, dc_rows], axis=1)
        dpadded, dkernel, doffsets = conv_pull(dmixed)
        spill = send(dpadded[: CONV - 1], "ctx", -1, layer)
        dconv = dpadded[CONV - 1 :] + jnp.pad(spill, ((tokens - (CONV - 1), 0), (0, 0)))
        dmix = dconv[:, :inner_local].astype(BF16)
        ddt_full = place_cols(ddt_raw.T, heads_total, tp_pos * heads_local, 1)
        dstate_part = jnp.concatenate([dconv[:, inner_local:], ddt_full], axis=1)
        dstate_part = lax.optimization_barrier(dstate_part.astype(BF16))
        dinput = jnp.concatenate([dgate, dmix, dstate_part], axis=1)
        dnormed_part = to_rows(dinput, input_weight).astype(BF16)
        summed = tp_sum(jnp.concatenate([dnormed_part, dstate_part], axis=1), layer)
        dnormed = summed[:, :width]
        dstate = summed[:, width:].astype(BF16)
        late = ((normed, dmix), (normed, dstate))
        if layer == 0:
            late_sum = own_rows(cross_grad(late, layer), layer)
            mats = jnp.concatenate([early_sum, late_sum], axis=1)
        else:
            mats = own_rows(cross_grad(early + late, layer), layer)
        _, norm_pull = jax.vjp(norm_apply, stream_in, norm_scale)
        dstream, dnorm_scale = norm_pull(dnormed)
        tp_first = (tp_pos == 0).astype(F32)
        smalls = (
            turned(dnorm_scale, width - turn, 0) * tp_first,
            place_cols(dkernel[:, :inner_local], inner_total, tp_pos * inner_local, 1),
            place_cols(doffsets[:inner_local], inner_total, tp_pos * inner_local, 0),
            dkernel[:, inner_local:],
            doffsets[inner_local:],
            place_cols(dstep, heads_total, tp_pos * heads_local, 0),
            place_cols(ddecay, heads_total, tp_pos * heads_local, 0),
            place_cols(dskip, heads_total, tp_pos * heads_local, 0),
            place_cols(dgate_scale, inner_total, tp_pos * inner_local, 0),
        )
        return (grad_out + dstream, mats, smalls)

    section_zero = section_pos == 0

    def pick_zero(from_zero, from_one):
        return jnp.where(section_zero, from_zero, from_one)

    input_zero = fetch(own_input, turn, 0)
    output_zero = fetch(own_output, input_zero[1:], 0)
    input_one = fetch(own_input, output_zero[1:], 1)
    output_one = fetch(own_output, input_one[1:], 1)
    weights_zero = (input_zero, output_zero)
    weights_one = (input_one, output_one)
    out_first, saved_first = forward(stream, weights_zero, 0)
    received = hand_over(out_first, 1)
    out_second, saved_second = forward(received, weights_one, 1)
    saved = jax.tree.map(pick_zero, saved_first, saved_second)
    cot_first = jnp.where(section_zero, jnp.zeros_like(stream), stream)
    grad_first, mats_first, small_first = backward(cot_first, saved, weights_one, 1)
    returned = hand_over(grad_first.astype(BF16), -1).astype(F32)
    grad_second, mats_second, small_second = backward(returned, saved, weights_zero, 0)
    mats = pick_zero(mats_second, mats_first)
    cuts = (inner_local, 2 * inner_local, 3 * inner_local)
    grad_output, grad_gate, grad_mix, grad_state = jnp.split(mats, cuts, axis=1)
    smalls = jax.tree.map(pick_zero, small_second, small_first)
    boundary_out = turned(jnp.where(section_zero, grad_second, out_second), width - turn, 1)
    flat = jnp.concatenate([value.reshape(-1) for value in smalls])
    flat = jnp.pad(flat, (0, -flat.shape[0] % 1024)).reshape(-1, 128)
    flat = all_sum(flat).reshape(-1)
    sums, start = [], 0
    for value in smalls:
        sums.append(flat[start : start + value.size].reshape((1,) + value.shape))
        start += value.size
    return (
        boundary_out[None, None],
        sums[0],
        jnp.stack([grad_gate, grad_mix], axis=1)[None],
        grad_state[None],
        *sums[1:],
        grad_output[None],
    )


def solution(mesh):
    in_specs = (
        P("section", "shard", "ctx", None),
        P("shard", None),
        P("section", None),
        P("section", "shard", None, "tp"),
        P("section", "shard", None),
        P("section", None, "tp"),
        P("section", "tp"),
        P("section", None, None),
        P("section", None),
        P("section", "tp"),
        P("section", "tp"),
        P("section", "tp"),
        P("section", "tp"),
        P("section", "shard", "tp"),
    )
    out_specs = (
        P("section", "shard", "ctx", None),
        P("section", None),
        P("section", ("shard", "ctx"), None, "tp"),
        P("section", ("shard", "ctx"), None),
        P("section", None, None),
        P("section", None),
        P("section", None, None),
        P("section", None),
        P("section", None),
        P("section", None),
        P("section", None),
        P("section", None),
        P("section", ("shard", "ctx"), "tp"),
    )
    return jax.shard_map(
        per_device, mesh=mesh, in_specs=in_specs, out_specs=out_specs, check_vma=False
    )
```

```python
import jax
import jax.numpy as jnp
from jax import lax
from jax.sharding import PartitionSpec as P

HEAD_DIM = 64
CONV = 4
LONGEST = 512
EPS = 1e-05
BF16 = jnp.bfloat16
F32 = jnp.float32
ROWS = (((0,), (0,)), ((), ()))
COLS = (((1,), (1,)), ((), ()))


def send(value, axis, shift, layer, wrap=False):
    count = lax.axis_size(axis)
    base = layer * count
    pairs = [
        (base + place, base + (place + shift) % count)
        for place in range(count)
        if wrap or 0 <= place + shift < count
    ]
    return lax.ppermute(value, ("section", axis), pairs)


def hand_over(value, steps):
    count = lax.axis_size("section")
    leading, last = (max(0, -steps), min(count, count - steps))
    return lax.ppermute(value, "section", [(place, place + steps) for place in range(leading, last)])


def tp_sum(value, layer):
    if lax.axis_size("tp") == 2:
        value = lax.optimization_barrier(value)
        return value.astype(F32) + send(value, "tp", 1, layer, True).astype(F32)
    return jnp.sum(lax.all_gather(value, "tp").astype(F32), axis=0)


def carried_in(decay, state, direction, layer):
    tokens = state[1]
    state = state[0]
    heads, _, width = state.shape
    reach = min(lax.axis_size("ctx") - 1, -(-(LONGEST - 1) // tokens))
    packed = jnp.concatenate(
        [state, jnp.broadcast_to(decay[:, None, None], (heads, 8, width))], axis=1
    ).astype(BF16)
    parts = [send(packed, "ctx", direction * (hop + 1), layer).astype(F32) for hop in range(reach)]
    total = jnp.zeros_like(state)
    for part in reversed(parts):
        total = part[:, :HEAD_DIM] + part[:, HEAD_DIM : HEAD_DIM + 1, :1] * total
    return total


def round_trip(values):
    narrow = lax.optimization_barrier(values.astype(BF16))
    return narrow.astype(F32)


def norm_apply(hidden, scale_vec):
    factor = lax.rsqrt(jnp.mean(hidden * hidden, axis=-1, keepdims=True) + EPS)
    return hidden * factor * scale_vec[None, :]


def conv_apply(padded, kernel, offsets, seg_pad):
    length = padded.shape[0] - (CONV - 1)
    current = seg_pad[CONV - 1 :]
    total = jnp.zeros((length, padded.shape[1]), F32) + offsets[None, :]
    for lag in range(CONV):
        same = (seg_pad[lag : lag + length] == current).astype(F32)
        total = total + kernel[lag][None, :] * padded[lag : lag + length] * same[:, None]
    return jax.nn.silu(total)


def gate_apply(ssd_flat, gate_vals, scale_vec):
    gated = ssd_flat * jax.nn.silu(gate_vals)
    return (gated * scale_vec[None, :], jnp.sum(gated * gated, axis=1))


def step_terms(dt_raw, step_vec, log_vec):
    tokens = dt_raw.shape[1]
    delta = jax.nn.softplus(dt_raw + step_vec[:, None])
    rates = -jnp.exp(log_vec)[:, None] * delta
    places = jnp.arange(tokens)
    upto = (places[:, None] <= places[None, :]).astype(F32)
    return delta, jnp.dot(rates, upto, precision=lax.Precision.HIGHEST)


def local_state(x_heads, b_rows, delta, cumul, segs):
    last_same = (segs == segs[-1])[None, :]
    tails = jnp.where(last_same, jnp.exp(cumul[:, -1:] - cumul), 0.0) * delta
    return jnp.einsum("hsp,sn->hpn", tails[:, :, None] * x_heads, b_rows)


def entries(cumul, segs, seg_before):
    return jnp.exp(cumul) * (segs == seg_before).astype(F32)[None, :]


def ssd_apply(
    x_heads, b_rows, c_rows, dt_raw, step_vec, log_vec, skip_vec, state_in, segs, seg_before
):
    tokens = x_heads.shape[1]
    delta, cumul = step_terms(dt_raw, step_vec, log_vec)
    places = jnp.arange(tokens)
    mask = ((places[:, None] >= places[None, :]) & (segs[:, None] == segs[None, :]))[None]
    spread = cumul[:, :, None] - cumul[:, None, :]
    decays = jnp.where(mask, jnp.exp(jnp.where(mask, spread, 0.0)), 0.0)
    scores = jnp.einsum("tn,sn->ts", c_rows, b_rows)
    mixing = scores[None] * decays * delta[:, None, :]
    inside = jnp.einsum("hts,hsp->htp", mixing, x_heads)
    reads = jnp.einsum("tn,hpn->htp", c_rows, state_in)
    carried = entries(cumul, segs, seg_before)[:, :, None] * reads
    result = inside + carried + skip_vec[:, None, None] * x_heads
    keeps = (segs[-1] == seg_before).astype(F32)
    block_decay = jnp.exp(cumul[:, -1]) * keeps
    final = block_decay[:, None, None] * state_in + local_state(
        x_heads, b_rows, delta, cumul, segs
    )
    return (result, final)


def cross_grad(pairs, layer):
    shards = lax.axis_size("shard")

    def part(index, kind):
        products = []
        for left, right in pairs:
            block = left.shape[1] // shards
            taken = left[:, index * block : (index + 1) * block]
            products.append(
                lax.dot_general(taken, right, ROWS, preferred_element_type=F32).astype(kind)
            )
        return jnp.concatenate(products, axis=1)

    away = [send(part(k, BF16), "shard", k, layer, True) for k in range(1, shards)]
    total = part(0, F32)
    for value in away:
        total = total + value.astype(F32)
    return total


def even_pairs(axis, distance, layer):
    count = lax.axis_size(axis)
    return [(layer * count + place, layer * count + (place ^ distance)) for place in range(count)]


def own_rows(total, layer):
    count = lax.axis_size("ctx")
    place = lax.axis_index("ctx")
    blocks = total.reshape(count, total.shape[0] // count, total.shape[1])
    if count & (count - 1):
        blocks = lax.psum_scatter(blocks.astype(BF16), "ctx", scatter_dimension=0, tiled=True)
        return blocks[0].astype(F32)
    distance = 1
    while distance < count:
        bit = lax.rem(place // distance, 2)
        pairs = blocks.reshape((blocks.shape[0] // 2, 2) + blocks.shape[1:])
        mine = lax.dynamic_index_in_dim(pairs, bit, 1, False)
        theirs = lax.dynamic_index_in_dim(pairs, 1 - bit, 1, False).astype(BF16)
        got = lax.ppermute(theirs, ("section", "ctx"), even_pairs("ctx", distance, layer))
        blocks = mine + got.astype(F32)
        distance *= 2
    return blocks[0]


def all_sum(value):
    for axis in ("shard", "ctx", "tp"):
        count = lax.axis_size(axis)
        if count & (count - 1):
            value = lax.psum(value, axis)
            continue
        distance = 1
        while distance < count:
            pairs = [(place, place ^ distance) for place in range(count)]
            value = value + lax.ppermute(value, axis, pairs)
            distance *= 2
    return value


def place_cols(values, full_width, start, axis_pos):
    shape_full = values.shape[:axis_pos] + (full_width,) + values.shape[axis_pos + 1 :]
    return lax.dynamic_update_slice_in_dim(jnp.zeros(shape_full, F32), values, start, axis_pos)


def turned(values, start, axis_pos):
    return lax.dynamic_slice_in_dim(
        jnp.concatenate([values, values], axis=axis_pos), start, values.shape[axis_pos], axis_pos
    )


def per_device(
    boundary,
    segments,
    norm_gain,
    inner_proj,
    state_proj,
    conv_inner,
    conv_inner_bias,
    conv_state,
    conv_state_bias,
    step_bias,
    decay_log,
    skip_gain,
    gate_gain,
    output_proj,
):
    section_pos = lax.axis_index("section")
    shard_pos = lax.axis_index("shard")
    shard_count = lax.axis_size("shard")
    ctx_pos = lax.axis_index("ctx")
    tp_pos = lax.axis_index("tp")
    tp_count = lax.axis_size("tp")
    tokens, width = boundary.shape[2:]
    rows = inner_proj.shape[1]
    heads_local = step_bias.shape[1]
    inner_local = conv_inner.shape[2]
    state_size = conv_state.shape[2] // 2
    heads_total = heads_local * tp_count
    inner_total = inner_local * tp_count
    turn = shard_pos * rows
    stream = turned(boundary[0, 0], turn, 1)
    norm_scale = turned(norm_gain[0], turn, 0)
    seq_all = segments[0]
    seg_pad = jnp.concatenate([jnp.full((CONV - 1,), -1, jnp.int32), seq_all])
    first_token = ctx_pos * tokens
    seg_ext = lax.dynamic_slice_in_dim(seg_pad, first_token, tokens + CONV - 1)
    seg_local = lax.dynamic_slice_in_dim(seq_all, first_token, tokens)
    seg_before = seg_ext[CONV - 2]
    keeps = (seg_local[-1] == seg_before).astype(F32)
    own_input = jnp.concatenate(
        [inner_proj[0, :, 0], inner_proj[0, :, 1], state_proj[0]], axis=1
    )
    own_output = output_proj[0]
    kernel = jnp.concatenate([conv_inner[0], conv_state[0]], axis=1)
    offsets = jnp.concatenate([conv_inner_bias[0], conv_state_bias[0]])
    step_vec = step_bias[0]
    log_vec = decay_log[0]
    skip_vec = skip_gain[0]
    gate_scale = gate_gain[0]

    def fetch(own, after, layer):
        sent, _ = lax.optimization_barrier((own, after))
        return [own] + [send(sent, "shard", -k, layer, True) for k in range(1, shard_count)]

    def by_rows(values, weight):
        total = None
        for k, part in enumerate(weight):
            product = jnp.dot(
                values[:, k * rows : (k + 1) * rows], part, preferred_element_type=F32
            )
            total = product if total is None else total + product
        return total

    def to_rows(values, weight):
        return jnp.concatenate(
            [lax.dot_general(values, part, COLS, preferred_element_type=F32) for part in weight],
            axis=1,
        )

    def split_mixed(mixed):
        x_heads = mixed[:, :inner_local].reshape(tokens, heads_local, HEAD_DIM)
        return (
            jnp.swapaxes(x_heads, 0, 1),
            mixed[:, inner_local : inner_local + state_size],
            mixed[:, inner_local + state_size :],
        )

    def flat_heads(values):
        return jnp.swapaxes(values, 0, 1).reshape(tokens, inner_local)

    def head_rows(values):
        return jnp.swapaxes(values.reshape(tokens, heads_local, HEAD_DIM), 0, 1)

    def ssd_local(x_in, b_in, c_in, raw_in, step_in, log_in, skip_in, state_start):
        return ssd_apply(
            x_in, b_in, c_in, raw_in, step_in, log_in, skip_in, state_start, seg_local, seg_before
        )

    def conv_local(values, kernel_all, offset_all):
        return conv_apply(values, kernel_all, offset_all, seg_ext)

    def forward(stream_in, weights, layer):
        input_weight, output_weight = weights
        normed = norm_apply(stream_in, norm_scale).astype(BF16)
        both = by_rows(normed, input_weight)
        inner_all = both[:, : 2 * inner_local].astype(BF16)
        state_all = both[:, 2 * inner_local :]
        dt_raw = lax.dynamic_slice_in_dim(
            state_all, 2 * state_size + tp_pos * heads_local, heads_local, 1
        ).T
        conv_input = jnp.concatenate(
            [inner_all[:, inner_local:], state_all[:, : 2 * state_size].astype(BF16)], axis=1
        )
        previous = send(conv_input[tokens - (CONV - 1) :], "ctx", 1, layer)
        padded = jnp.concatenate([previous, conv_input], axis=0)
        mixed = round_trip(conv_apply(padded.astype(F32), kernel, offsets, seg_ext))
        x_heads, b_rows, c_rows = split_mixed(mixed)
        delta, cumul = step_terms(dt_raw, step_vec, log_vec)
        decay = jnp.exp(cumul[:, -1]) * keeps
        state = local_state(x_heads, b_rows, delta, cumul, seg_local)
        state_in = carried_in(decay, (state, tokens), 1, layer)
        ssd_out, _ = ssd_local(
            x_heads, b_rows, c_rows, dt_raw, step_vec, log_vec, skip_vec, state_in
        )
        vpre, squares = gate_apply(
            flat_heads(ssd_out), inner_all[:, :inner_local].astype(F32), gate_scale
        )
        vproj = vpre.astype(BF16)
        high = lax.optimization_barrier(squares.astype(BF16))
        low = (squares - high.astype(F32)).astype(BF16)
        ends = jnp.pad(jnp.stack([high, low], axis=1), ((0, 0), (0, 126)))
        summed = tp_sum(
            jnp.concatenate([to_rows(vproj, output_weight).astype(BF16), ends], axis=1), layer
        )
        proj = summed[:, :width]
        squares_sum = summed[:, width] + summed[:, width + 1]
        rstd = lax.rsqrt(squares_sum / inner_total + EPS)
        output = stream_in + rstd[:, None] * proj
        return (
            output,
            (stream_in, normed, inner_all, padded, dt_raw, state_in, decay, vproj, proj, rstd),
        )

    def backward(grad_out, saved, weights, layer, done=None):
        input_weight, output_weight = weights
        stream_in, normed, inner_all, padded, dt_raw, state_in, decay, vproj, proj, rstd = saved
        dproj = (rstd[:, None] * grad_out).astype(BF16)
        drstd = jnp.sum(grad_out * proj, axis=1)
        dvpre = by_rows(dproj, output_weight)
        dsquares = -0.5 * drstd * rstd * rstd * rstd / inner_total
        mixed_raw, conv_pull = jax.vjp(conv_local, padded.astype(F32), kernel, offsets)
        x_heads, b_rows, c_rows = split_mixed(round_trip(mixed_raw))
        (ssd_out, _), ssd_pull = jax.vjp(
            ssd_local, x_heads, b_rows, c_rows, dt_raw, step_vec, log_vec, skip_vec, state_in
        )
        _, gate_pull = jax.vjp(
            gate_apply, flat_heads(ssd_out), inner_all[:, :inner_local].astype(F32), gate_scale
        )
        dssd, dgate_in, dgate_scale = gate_pull((dvpre, dsquares))
        dgate = dgate_in.astype(BF16)
        early = ((dproj, vproj), (normed, dgate))
        if layer == 0:
            early_sum = own_rows(cross_grad(early, layer), layer)
        dssd_heads = head_rows(dssd)
        _, cumul = step_terms(dt_raw, step_vec, log_vec)
        entry = entries(cumul, seg_local, seg_before)
        local_grad = jnp.einsum("tn,htp->hpn", c_rows, entry[:, :, None] * dssd_heads)
        state_grad = carried_in(decay, (local_grad, tokens), -1, layer)
        dx_heads, db_rows, dc_rows, ddt_raw, dstep, ddecay, dskip, _ = ssd_pull(
            (dssd_heads, state_grad)
        )
        dmixed = jnp.concatenate([flat_heads(dx_heads), db_rows, dc_rows], axis=1)
        dpadded, dkernel, doffsets = conv_pull(dmixed)
        spill = send(dpadded[: CONV - 1], "ctx", -1, layer)
        dconv = dpadded[CONV - 1 :] + jnp.pad(spill, ((tokens - (CONV - 1), 0), (0, 0)))
        dmix = dconv[:, :inner_local].astype(BF16)
        ddt_full = place_cols(ddt_raw.T, heads_total, tp_pos * heads_local, 1)
        dstate_part = jnp.concatenate([dconv[:, inner_local:], ddt_full], axis=1)
        dstate_part = lax.optimization_barrier(dstate_part.astype(BF16))
        dinput = jnp.concatenate([dgate, dmix, dstate_part], axis=1)
        dnormed_part = to_rows(dinput, input_weight).astype(BF16)
        summed = tp_sum(jnp.concatenate([dnormed_part, dstate_part], axis=1), layer)
        dnormed = summed[:, :width]
        dstate = summed[:, width:].astype(BF16)
        late = ((normed, dmix), (normed, dstate))
        if layer == 0:
            tied, _ = lax.optimization_barrier((late, done))
            late = tied
            late_sum = own_rows(cross_grad(late, layer), layer)
            mats = jnp.concatenate([early_sum, late_sum], axis=1)
        else:
            mats = own_rows(cross_grad(early + late, layer), layer)
        _, norm_pull = jax.vjp(norm_apply, stream_in, norm_scale)
        dstream, dnorm_scale = norm_pull(dnormed)
        tp_first = (tp_pos == 0).astype(F32)
        smalls = (
            turned(dnorm_scale, width - turn, 0) * tp_first,
            place_cols(dkernel[:, :inner_local], inner_total, tp_pos * inner_local, 1),
            place_cols(doffsets[:inner_local], inner_total, tp_pos * inner_local, 0),
            dkernel[:, inner_local:],
            doffsets[inner_local:],
            place_cols(dstep, heads_total, tp_pos * heads_local, 0),
            place_cols(ddecay, heads_total, tp_pos * heads_local, 0),
            place_cols(dskip, heads_total, tp_pos * heads_local, 0),
            place_cols(dgate_scale, inner_total, tp_pos * inner_local, 0),
        )
        return (grad_out + dstream, mats, smalls)

    section_zero = section_pos == 0

    def pick_zero(from_zero, from_one):
        return jnp.where(section_zero, from_zero, from_one)

    input_zero = fetch(own_input, turn, 0)
    output_zero = fetch(own_output, input_zero[1:], 0)
    input_one = fetch(own_input, output_zero[1:], 1)
    output_one = fetch(own_output, input_one[1:], 1)
    weights_zero = (input_zero, output_zero)
    weights_one = (input_one, output_one)
    out_first, saved_first = forward(stream, weights_zero, 0)
    received = hand_over(out_first, 1)
    out_second, saved_second = forward(received, weights_one, 1)
    saved = jax.tree.map(pick_zero, saved_first, saved_second)
    cot_first = jnp.where(section_zero, jnp.zeros_like(stream), stream)
    grad_first, mats_first, small_first = backward(cot_first, saved, weights_one, 1)
    returned = hand_over(grad_first.astype(BF16), -1).astype(F32)
    grad_second, mats_second, small_second = backward(returned, saved, weights_zero, 0, mats_first)
    mats = pick_zero(mats_second, mats_first)
    cuts = (inner_local, 2 * inner_local, 3 * inner_local)
    grad_output, grad_gate, grad_mix, grad_state = jnp.split(mats, cuts, axis=1)
    smalls = jax.tree.map(pick_zero, small_second, small_first)
    boundary_out = turned(jnp.where(section_zero, grad_second, out_second), width - turn, 1)
    flat = jnp.concatenate([value.reshape(-1) for value in smalls])
    flat = jnp.pad(flat, (0, -flat.shape[0] % 1024)).reshape(-1, 128)
    flat = all_sum(flat).reshape(-1)
    sums, start = [], 0
    for value in smalls:
        sums.append(flat[start : start + value.size].reshape((1,) + value.shape))
        start += value.size
    return (
        boundary_out[None, None],
        sums[0],
        jnp.stack([grad_gate, grad_mix], axis=1)[None],
        grad_state[None],
        *sums[1:],
        grad_output[None],
    )


def solution(mesh):
    in_specs = (
        P("section", "shard", "ctx", None),
        P("shard", None),
        P("section", None),
        P("section", "shard", None, "tp"),
        P("section", "shard", None),
        P("section", None, "tp"),
        P("section", "tp"),
        P("section", None, None),
        P("section", None),
        P("section", "tp"),
        P("section", "tp"),
        P("section", "tp"),
        P("section", "tp"),
        P("section", "shard", "tp"),
    )
    out_specs = (
        P("section", "shard", "ctx", None),
        P("section", None),
        P("section", ("shard", "ctx"), None, "tp"),
        P("section", ("shard", "ctx"), None),
        P("section", None, None),
        P("section", None),
        P("section", None, None),
        P("section", None),
        P("section", None),
        P("section", None),
        P("section", None),
        P("section", None),
        P("section", ("shard", "ctx"), "tp"),
    )
    return jax.shard_map(
        per_device, mesh=mesh, in_specs=in_specs, out_specs=out_specs, check_vma=False
    )
```
